1024 devices in a mesh: dp: 16 (over z), space: 64 (over y, x, core).
Axes of the slice: x: 4, y: 8, z: 16, core: 2. Of those that a mesh axis runs over, the one named last changes fastest.
Arguments:
- activations: bfloat16 [16, 128, 180, 768], P('dp', 'space'), may hold values from -6 to 6
- cotangent: bfloat16 [16, 128, 180, 768], P('dp', 'space'), may hold values from -6 to 6
- w_first: bfloat16 [2, 768, 96], replicated, may hold values from -0.4375 to 0.4375
- w_second: bfloat16 [2, 768, 96], replicated, may hold values from -0.4375 to 0.4375
- b_first: float32 [2, 768], replicated, may hold values from -3 to 3
- lon_keep: int32 [64], replicated, may hold values from 0 to 90, as said below
- relu_mask: int32 [16, 128, 2, 64, 768], P('dp', None, None, 'space'), may hold values 0 or 1
- shrink_mask: int32 [16, 128, 2, 64, 768], P('dp', None, None, 'space'), may hold values 0 or 1
Outputs:
- grad_activations: bfloat16 [16, 128, 180, 768], P('dp', 'space')
- grad_w_first: float32 [2, 768, 96], P(None, 'dp')
- grad_w_second: float32 [2, 768, 96], P(None, 'dp')
- grad_b_first: float32 [2, 768], P(None, 'dp')
- grad_b_second: float32 [2, 768], P(None, 'dp')
The draws below stay inside these ranges and needn't reach their ends.
Inputs may be any that keep to these rules, and one draw needn't show every extreme that they name: `lon_keep`: 64 distinct longitude frequencies, 0 and 90 among them, in no particular order.
All inputs are finite; a program needn't handle non-finite values. No bound on the sum of `relu_mask` or of `shrink_mask` on one device may be relied on, other than what follows from the above.
Results may differ from the reference program's by a relative error of at most 0.011.
Values may be sent and summed in bfloat16 or wider, within the bound.
A program may use at most 32 MiB of HBM per device.

```python
import math
import jax
import jax.numpy as jnp
from jax import lax

C = 768
BLOCKS = 8
LON = 180
BS = 96
SAMPLES = 16
LAT = 128
KW = 64


def draw_lon_keep(key, part):
    middle = jax.random.permutation(key, jnp.arange(1, LON // 2, dtype=jnp.int32))[:KW - 2]
    values = jnp.concatenate([jnp.array([0, LON // 2], dtype=jnp.int32), middle])
    return jax.random.permutation(jax.random.fold_in(key, 7), values)


def touch_ends(values, rng, low, largest):
    index_at = [jax.random.randint(jax.random.fold_in(rng, axis), (), 0, length) for axis, length in enumerate(values.shape)]
    main_axis = values.shape.index(max(values.shape))
    neighbour = index_at[:main_axis] + [(index_at[main_axis] + 1) % values.shape[main_axis]] + index_at[main_axis + 1:]
    return values.at[tuple(index_at)].set(low).at[tuple(neighbour)].set(largest)


def levels(rng, extent, split, smallest, top_value):
    loudness, own = 1.0, jax.random.fold_in(rng, 6)
    for axis_at, blocks in split:
        draws = jnp.exp(jax.random.uniform(jax.random.fold_in(own, axis_at), (blocks,), jnp.float32, smallest / len(split), top_value / len(split)))
        loudness = loudness * jnp.repeat(draws, extent[axis_at] // blocks).reshape([-1 if axis == axis_at else 1 for axis in range(len(extent))])
    return loudness


def noise(rng, shape, width, most, shards=(), held_as=jnp.bfloat16):
    loudness = levels(rng, shape, shards, -0.22, 0.18) if shards else 1.0
    result = jax.random.normal(rng, shape, jnp.float32) * width * loudness
    return jnp.minimum(jnp.maximum(result, -most), most).astype(held_as)


def setup_inputs(seed: int = 0) -> dict:
    key_list = jax.random.split(jax.random.key(seed), 9)
    return {
        "activations": noise(key_list[0], (SAMPLES, LAT, LON, C), 1.0, 6.0, ((0, 16), (1, 64))),
        "cotangent": noise(key_list[1], (SAMPLES, LAT, LON, C), 1.0, 6.0, ((0, 16), (1, 64))),
        "w_first": noise(key_list[2], (2, C, BS), (2 * BS) ** -0.5, 0.4375),
        "w_second": noise(key_list[3], (2, C, BS), (2 * BS) ** -0.5, 0.4375),
        "b_first": noise(key_list[4], (2, C), 0.5, 3.0, (), jnp.float32),
        "lon_keep": draw_lon_keep(jax.random.fold_in(key_list[8], 71), 0),
        "relu_mask": touch_ends((jax.random.randint(key_list[6], (SAMPLES, LAT, 2, KW, C), 0, 2) < 1).astype(jnp.int32), jax.random.fold_in(key_list[6], 1), 0, 1),
        "shrink_mask": touch_ends((jax.random.randint(key_list[7], (SAMPLES, LAT, 2, KW, C), 0, 4) < 3).astype(jnp.int32), jax.random.fold_in(key_list[7], 1), 0, 1),
    }


def build_tables(lon_keep, lat_len, lon_len):
    columns = jnp.arange(lon_len, dtype=jnp.int32)
    lon_phase = columns[:, None] * lon_keep[None, :] % lon_len
    lon_angle = lon_phase.astype(jnp.float32) * (2.0 * math.pi / lon_len)
    lon_table = jnp.stack([jnp.cos(lon_angle), -jnp.sin(lon_angle)], axis=1).astype(jnp.bfloat16)
    latitudes = jnp.arange(lat_len, dtype=jnp.int32)
    lat_phase = latitudes[:, None] * latitudes[None, :] % lat_len
    lat_angle = lat_phase.astype(jnp.float32) * (2.0 * math.pi / lat_len)
    cosine = jnp.cos(lat_angle)
    sine_part = jnp.sin(lat_angle)
    lat_table = jnp.stack([jnp.stack([cosine, sine_part], axis=-1), jnp.stack([-sine_part, cosine], axis=-1)], axis=1).astype(jnp.bfloat16)
    return (lon_table, lat_table)

def apply_blocks(operand, matrix):
    return jnp.einsum('mkbc,bcd->mkbd', operand.astype(jnp.float32), matrix.astype(jnp.float32))

def adjoint(operand, matrix):
    return jnp.einsum('mkbd,bcd->mkbc', operand.astype(jnp.float32), matrix.astype(jnp.float32))

def outer_sum(operand, other):
    return jnp.einsum('mkbc,mkbd->bcd', operand.astype(jnp.float32), other.astype(jnp.float32))

def reference(activations, cotangent, w_first, w_second, b_first, lon_keep, relu_mask, shrink_mask):
    lon_table, lat_table = build_tables(lon_keep, LAT, LON)
    lon_wide = lon_table.astype(jnp.float32)
    lat_wide = lat_table.astype(jnp.float32)
    ortho_scale = 1.0 / math.sqrt(LAT * LON)
    doubled = jnp.where((lon_keep == 0) | (2 * lon_keep == LON), 1.0, 2.0).astype(jnp.float32)
    first_blocks = w_first.reshape(2, BLOCKS, BS, BS)
    second_blocks = w_second.reshape(2, BLOCKS, BS, BS)
    bias_blocks = b_first.reshape(2, BLOCKS, BS)

    def spectrum(field_in):
        along_lon = jnp.einsum('hwc,wpk->hpkc', field_in.astype(jnp.float32), lon_wide).astype(jnp.bfloat16)
        return (jnp.einsum('mphq,hqkc->mpkc', lat_wide, along_lon.astype(jnp.float32)) * ortho_scale).astype(jnp.bfloat16)

    def blocked(array):
        return array.reshape(LAT, 2, KW, BLOCKS, BS)

    def one_sample(totals, inputs):
        field_in, tangent, relu_bits, shrink_bits = inputs
        spec_act = blocked(spectrum(field_in))
        spec_cot = spectrum(tangent)
        relu_gate = blocked(relu_bits) > 0
        grad_out = blocked(jnp.where(shrink_bits > 0, doubled[None, None, :, None] * spec_cot.astype(jnp.float32), 0.0).astype(jnp.bfloat16))
        act_real = spec_act[:, 0]
        act_imag = spec_act[:, 1]
        pre_real = apply_blocks(act_real, first_blocks[0]) - apply_blocks(act_imag, first_blocks[1]) + bias_blocks[0]
        pre_imag = apply_blocks(act_real, first_blocks[1]) + apply_blocks(act_imag, first_blocks[0]) + bias_blocks[1]
        hidden = jnp.where(relu_gate, jnp.stack([pre_real, pre_imag], axis=1), 0.0).astype(jnp.bfloat16)
        out_real = grad_out[:, 0]
        out_imag = grad_out[:, 1]
        hidden_real = adjoint(out_real, second_blocks[0]) + adjoint(out_imag, second_blocks[1])
        hidden_imag = -adjoint(out_real, second_blocks[1]) + adjoint(out_imag, second_blocks[0])
        grad_pre = jnp.where(relu_gate, jnp.stack([hidden_real, hidden_imag], axis=1), 0.0).astype(jnp.bfloat16)
        pre_grad_real = grad_pre[:, 0]
        pre_grad_imag = grad_pre[:, 1]
        spec_real = adjoint(pre_grad_real, first_blocks[0]) + adjoint(pre_grad_imag, first_blocks[1])
        spec_imag = -adjoint(pre_grad_real, first_blocks[1]) + adjoint(pre_grad_imag, first_blocks[0])
        grad_spec = jnp.stack([spec_real, spec_imag], axis=1).astype(jnp.bfloat16).reshape(LAT, 2, KW, C)
        first_grad = jnp.stack([outer_sum(act_real, pre_grad_real) + outer_sum(act_imag, pre_grad_imag), outer_sum(act_real, pre_grad_imag) - outer_sum(act_imag, pre_grad_real)])
        hid_real = hidden[:, 0]
        hid_imag = hidden[:, 1]
        second_grad = jnp.stack([outer_sum(hid_real, out_real) + outer_sum(hid_imag, out_imag), outer_sum(hid_real, out_imag) - outer_sum(hid_imag, out_real)])
        bias_first = lax.optimization_barrier(jnp.sum(grad_pre, axis=(0, 2), dtype=jnp.float32))
        bias_second = lax.optimization_barrier(jnp.sum(grad_out, axis=(0, 2), dtype=jnp.float32))
        grad_lat = jnp.einsum('mqhp,mqkc->hpkc', lat_wide, grad_spec.astype(jnp.float32)).astype(jnp.bfloat16)
        grad_field = (jnp.einsum('wpk,hpkc->hwc', lon_wide, grad_lat.astype(jnp.float32)) * ortho_scale).astype(jnp.bfloat16)
        updated = (totals[0] + first_grad, totals[1] + second_grad, totals[2] + bias_first, totals[3] + bias_second)
        return (updated, grad_field)
    start_totals = (jnp.zeros((2, BLOCKS, BS, BS), jnp.float32), jnp.zeros((2, BLOCKS, BS, BS), jnp.float32), jnp.zeros((2, BLOCKS, BS), jnp.float32), jnp.zeros((2, BLOCKS, BS), jnp.float32))
    totals, grad_fields = lax.scan(one_sample, start_totals, (activations, cotangent, relu_mask, shrink_mask))
    grad_norm = 1.0 / math.sqrt(SAMPLES * LAT * KW)
    return (grad_fields, (totals[0] * grad_norm).reshape(2, C, BS), (totals[1] * grad_norm).reshape(2, C, BS), (totals[2] * grad_norm).reshape(2, C), (totals[3] * grad_norm).reshape(2, C))
```

```python
import functools
import math

import jax
import jax.numpy as jnp
import ml_dtypes
import numpy as np
from jax import lax
from jax.experimental import pallas as pl
from jax.experimental.pallas import tpu as pltpu
from jax.sharding import PartitionSpec as P

C = 768
BLOCKS = 8
LON = 180
BS = 96
HALF = C // 2
LANES = 128
NX = 4
ROWS = 8
TILES = 20
PIECE = TILES // NX
MESH = pl.DeviceIdType.MESH
F32 = jnp.float32
BF16 = jnp.bfloat16
WIRE = BF16


def lat_constant(lat_len):
    index = np.arange(lat_len)
    angle = ((index[:, None] * index[None, :]) % lat_len) * (2.0 * math.pi / lat_len)
    cosine, sine = np.cos(angle), np.sin(angle)
    table = np.stack(
        [np.stack([cosine, sine], -1), np.stack([-sine, cosine], -1)], 1
    )
    table = table.transpose(1, 0, 2, 3).reshape(2 * lat_len, lat_len // 2, 4)
    wide = np.zeros((2, 2 * lat_len, lat_len // 2, 2, 4))
    for part in range(2):
        wide[part, :, :, part, :] = table
    wide = wide.reshape(2, 2 * lat_len, 4 * lat_len).astype(ml_dtypes.bfloat16)
    return wide, np.ascontiguousarray(wide.transpose(0, 2, 1))


def lon_constant():
    columns, freq = np.arange(LON), np.arange(LON // 2 + 1)
    phase = (columns[:, None] * freq[None, :]) % LON
    angle = phase.astype(np.float32) * np.float32(2.0 * math.pi / LON)
    table = np.zeros((LON, 2, 2, 2, LANES))
    for row in range(2):
        table[:, row, row, 0, : LON // 2 + 1] = np.cos(angle)
        table[:, row, row, 1, : LON // 2 + 1] = -np.sin(angle)
    return table.reshape(2 * LON, 4 * LANES).astype(ml_dtypes.bfloat16)


def spread_constant():
    spread = np.zeros((HALF, 4 * LANES))
    for block in range(4):
        for channel in range(BS):
            spread[block * BS + channel, block * LANES + channel] = 1.0
    return spread.astype(ml_dtypes.bfloat16)


def dot(lhs, rhs, lhs_dim=1, rhs_dim=0):
    return lax.dot_general(
        lhs, rhs, (((lhs_dim,), (rhs_dim,)), ((), ())), preferred_element_type=F32
    )


def kernel(
    n_dp,
    n_space,
    keep_s,
    keep_v,
    act_h,
    cot_h,
    w1_h,
    w2_h,
    bias_h,
    relu_h,
    shrink_h,
    lonc_h,
    latf_h,
    latb_h,
    spread_h,
    out_field,
    out_w1,
    out_w2,
    out_b1,
    out_b2,
    x_v,
    relu_v,
    shrink_v,
    w_v,
    bias_v,
    lonc_v,
    latf_v,
    latb_v,
    spread_v,
    load_sem,
    inv_v,
    rmask,
    smask,
    wmat,
    bias_p,
    send_f,
    recv_f,
    gspec,
    send_b,
    recv_b,
    chunks,
    recv_c,
    send_x,
    recv_x,
    send_z,
    recv_z,
    recv_y,
    recv_g,
    sem_fs,
    sem_fr,
    sem_bs,
    sem_br,
    sem_cs,
    sem_cr,
    sem_xs,
    sem_xr,
    sem_zs,
    sem_zr,
    sem_ys,
    sem_yr,
    sem_gs,
    sem_gr,
    sem_own,
):
    lat_len = 2 * n_space
    n_y = n_space // (2 * NX)
    scale = 1.0 / math.sqrt(lat_len * LON)
    norm = 1.0 / math.sqrt(n_dp * lat_len * n_space)
    z = lax.axis_index("dp")
    me = lax.axis_index("space")
    core = lax.rem(me, 2)
    x = lax.rem(me // 2, NX)
    y = me // (2 * NX)
    barrier = pltpu.get_barrier_semaphore()

    def greet_space(k, carry):
        peer = lax.rem(me + k, n_space)
        pl.semaphore_signal(barrier, inc=1, device_id={"space": peer}, device_id_type=MESH)
        return carry

    def greet_dp(k, carry):
        peer = lax.rem(z + k, n_dp)
        pl.semaphore_signal(barrier, inc=1, device_id={"dp": peer}, device_id_type=MESH)
        return carry

    loads = [
        pltpu.make_async_copy(lonc_h, lonc_v, load_sem.at[0]),
        pltpu.make_async_copy(act_h, x_v.at[0], load_sem.at[1]),
        pltpu.make_async_copy(cot_h, x_v.at[1], load_sem.at[2]),
        pltpu.make_async_copy(spread_h, spread_v, load_sem.at[3]),
        pltpu.make_async_copy(relu_h, relu_v, load_sem.at[4]),
        pltpu.make_async_copy(shrink_h, shrink_v, load_sem.at[5]),
        pltpu.make_async_copy(w1_h, w_v.at[0], load_sem.at[6]),
        pltpu.make_async_copy(w2_h, w_v.at[1], load_sem.at[7]),
        pltpu.make_async_copy(bias_h, bias_v, load_sem.at[8]),
        pltpu.make_async_copy(latf_h, latf_v, load_sem.at[9]),
        pltpu.make_async_copy(latb_h, latb_v, load_sem.at[10]),
    ]
    for load in loads:
        load.start()
    lax.fori_loop(1, n_space, greet_space, 0)
    lax.fori_loop(1, n_dp, greet_dp, 0)

    rows = 8 * n_space
    freq = lax.broadcasted_iota(jnp.int32, (LANES, n_space), 0)
    picked = jnp.where(freq == keep_v[...], 1.0, 0.0).astype(BF16)
    row_mode = lax.broadcasted_iota(jnp.int32, (rows, n_space), 0) // 8
    mode = lax.broadcasted_iota(jnp.int32, (rows, n_space), 1)
    repeat = jnp.where(row_mode == mode, 1.0, 0.0).astype(BF16)
    one_hot = dot(repeat, picked, 1, 1)
    row_kind = lax.rem(lax.broadcasted_iota(jnp.int32, (rows, LANES), 0), 4)
    one_hot = jnp.concatenate(
        [jnp.where(row_kind == kind, one_hot, 0.0) for kind in range(4)], axis=1
    ).astype(BF16)
    loads[0].wait()
    lon_fwd = dot(one_hot, lonc_v[...], 1, 1)
    row_group = lax.rem(lax.broadcasted_iota(jnp.int32, (rows, 2 * LON), 0) // 4, 2)
    total = None
    for part in range(2):
        loads[1 + part].wait()
        table = jnp.where(row_group == part, lon_fwd, 0.0).astype(BF16)
        term = dot(table, x_v[part].reshape(2 * LON, C))
        total = term if total is None else total + term
    send_f[...] = total.astype(BF16).reshape(n_space, 8, C)

    pl.semaphore_wait(barrier, n_space + n_dp - 2)

    def push_forward(k, carry):
        peer = lax.rem(me + k, n_space)
        pltpu.make_async_remote_copy(
            src_ref=send_f.at[peer],
            dst_ref=recv_f.at[me],
            send_sem=sem_fs,
            recv_sem=sem_fr,
            device_id={"space": peer},
            device_id_type=MESH,
        ).start()
        return carry

    lax.fori_loop(1, n_space, push_forward, 0)
    own_f = pltpu.make_async_copy(send_f.at[me], recv_f.at[me], sem_own.at[0])
    own_f.start()

    lon_inv = dot(lonc_v[...], one_hot, 1, 1)
    col_group = lax.rem(lax.broadcasted_iota(jnp.int32, (2 * LON, rows), 1) // 4, 2)
    for half in range(2):
        inv_v[half] = jnp.where(col_group == half, lon_inv, 0.0).astype(BF16)
    loads[3].wait()
    spread = spread_v[...]
    for load, source, target in ((loads[4], relu_v, rmask), (loads[5], shrink_v, smask)):
        load.wait()
        for part in range(2):
            for half in range(2):
                tiles = [
                    source[pl.ds(part * 6 + half * 3 + tile, lat_len, stride=12), :]
                    for tile in range(3)
                ]
                bits = jnp.concatenate(tiles, axis=1)
                bits = jnp.where(bits > 0, 1.0, 0.0).astype(BF16)
                wide = dot(bits, spread)
                for block in range(4):
                    target[:, pl.ds((half * 4 + block) * 256 + part * LANES, LANES)] = wide[
                        :, block * LANES : (block + 1) * LANES
                    ]
    wmat[...] = jnp.zeros_like(wmat)
    for which in range(2):
        loads[6 + which].wait()
        for part in range(2):
            for half in range(2):
                wide = dot(
                    w_v[which, part, :, half * HALF : (half + 1) * HALF], spread
                )
                for block in range(4):
                    tile = wide[:, block * LANES : (block + 1) * LANES].astype(BF16)
                    at = half * 4 + block
                    if part == 0:
                        wmat[which, at, 0:BS, 0:LANES] = tile
                        wmat[which, at, LANES : LANES + BS, LANES:] = tile
                    else:
                        wmat[which, at, LANES : LANES + BS, 0:LANES] = tile
                        wmat[which, at, 0:BS, LANES:] = -tile
    loads[8].wait()
    spread_wide = spread.astype(F32)
    for part in range(2):
        for half in range(2):
            row = jnp.broadcast_to(
                bias_v[part : part + 1, half * HALF : (half + 1) * HALF], (8, HALF)
            )
            wide = lax.dot_general(
                row,
                spread_wide,
                (((1,), (0,)), ((), ())),
                precision=lax.Precision.HIGHEST,
                preferred_element_type=F32,
            )
            for block in range(4):
                bias_p[:, pl.ds((half * 4 + block) * 256 + part * LANES, LANES)] = wide[
                    :, block * LANES : (block + 1) * LANES
                ]
    loads[9].wait()
    loads[10].wait()
    own_keep = keep_s[me]
    weight = jnp.where((own_keep == 0) | (2 * own_keep == LON), 1.0, 2.0).astype(F32)

    own_f.wait()
    others = recv_f.at[pl.ds(0, n_space - 1)]
    pltpu.make_async_copy(others, others, sem_fr).wait()

    modes = recv_f[...].reshape(rows, C)
    lane = lax.broadcasted_iota(jnp.int32, (BS, LANES), 1)
    lane8 = lax.broadcasted_iota(jnp.int32, (8, LANES), 1)
    row8 = lax.broadcasted_iota(jnp.int32, (8, LANES), 0)
    spec = [(dot(latf_v[part], modes) * scale).astype(BF16) for part in range(2)]

    def packed(values, lanes):
        first = pltpu.roll(values[1], 96, 1)
        second = pltpu.roll(values[2], 64, 1)
        third = pltpu.roll(values[3], 32, 1)
        return (
            jnp.where(lanes < 96, values[0], first),
            jnp.where(lanes < 64, first, second),
            jnp.where(lanes < 32, second, third),
        )

    for half in range(2):
        cut = slice(half * HALF, (half + 1) * HALF)
        wide_act = dot(spec[0][:, cut], spread).astype(BF16)
        wide_cot = dot(spec[1][:, cut], spread)
        for block in range(4):
            at = half * 4 + block
            lanes = slice(block * LANES, (block + 1) * LANES)
            span = slice(at * 256, (at + 1) * 256)
            zed = jnp.concatenate(
                [wide_act[0:lat_len, lanes], wide_act[lat_len:, lanes]], axis=1
            )
            cot = jnp.concatenate(
                [wide_cot[0:lat_len, lanes], wide_cot[lat_len:, lanes]], axis=1
            )
            gate = rmask[:, span] > 0.5
            grad_out = jnp.where(smask[:, span] > 0.5, weight * cot, 0.0).astype(BF16)
            pre = dot(zed, wmat[0, at], 1, 1) + bias_p[0:1, span]
            hidden = jnp.where(gate, pre, 0.0).astype(BF16)
            grad_hidden = dot(grad_out, wmat[1, at])
            grad_pre = jnp.where(gate, grad_hidden, 0.0).astype(BF16)
            grad_spec = dot(grad_pre, wmat[0, at]).astype(BF16)
            gspec[0:lat_len, pl.ds(at * LANES, LANES)] = grad_spec[:, 0:LANES]
            gspec[lat_len:, pl.ds(at * LANES, LANES)] = grad_spec[:, LANES:]
            outer = []
            for left, right in ((zed, grad_pre), (hidden, grad_out)):
                full = dot(left, right, 0, 0)
                outer.append(full[0:BS, 0:LANES] + full[LANES : LANES + BS, LANES:])
                outer.append(full[0:BS, LANES:] - full[LANES : LANES + BS, 0:LANES])
            tiles = packed(outer, lane)
            for parity in range(2):
                for group in range(6):
                    for which in range(3):
                        tile = group * 3 + which
                        start = parity * 48 + group * 8
                        chunks[parity, tile // PIECE, at, tile % PIECE] = tiles[which][
                            start : start + 8
                        ]
            sums = []
            for value in (grad_pre, grad_out):
                line = jnp.sum(value.astype(F32), axis=0, keepdims=True)
                sums.append(jnp.broadcast_to(line[:, 0:LANES], (8, LANES)))
                sums.append(jnp.broadcast_to(line[:, LANES:], (8, LANES)))
            lines = packed(sums, lane8)
            tile = jnp.where(
                row8 == 0, lines[0], jnp.where(row8 == 1, lines[1], jnp.where(row8 == 2, lines[2], 0.0))
            )
            for parity in range(2):
                chunks[parity, 18 // PIECE, at, 18 % PIECE] = tile
                chunks[parity, 19 // PIECE, at, 19 % PIECE] = jnp.zeros((8, LANES), F32)

    sibling = me + 1 - 2 * core
    core_copies = []
    for step in range(NX):
        piece = lax.rem(x + 1 + step, NX)
        copy = pltpu.make_async_remote_copy(
            src_ref=chunks.at[1 - core, piece],
            dst_ref=recv_c.at[piece],
            send_sem=sem_cs.at[step],
            recv_sem=sem_cr.at[step],
            device_id={"space": sibling},
            device_id_type=MESH,
        )
        copy.start()
        core_copies.append(copy)

    grad_lat = None
    for half in range(2):
        narrow = dot(gspec[:, half * 512 : (half + 1) * 512], spread, 1, 1).astype(BF16)
        term = dot(latb_v[half], narrow)
        grad_lat = term if grad_lat is None else grad_lat + term
    send_b[...] = grad_lat.astype(BF16).reshape(n_space, 8, HALF)

    def push_back(k, carry):
        peer = lax.rem(me + k, n_space)
        pltpu.make_async_remote_copy(
            src_ref=send_b.at[peer],
            dst_ref=recv_b.at[me],
            send_sem=sem_bs,
            recv_sem=sem_br,
            device_id={"space": peer},
            device_id_type=MESH,
        ).start()
        return carry

    lax.fori_loop(1, n_space, push_back, 0)
    own_b = pltpu.make_async_copy(send_b.at[me], recv_b.at[me], sem_own.at[1])
    own_b.start()

    for step in range(NX):
        piece = lax.rem(x + 1 + step, NX)
        core_copies[step].wait()
        both = chunks[core, piece] + recv_c[piece]
        if step < NX - 1:
            send_x[step] = both.astype(WIRE)
            pltpu.make_async_remote_copy(
                src_ref=send_x.at[step],
                dst_ref=recv_x.at[NX - 2 - step],
                send_sem=sem_xs,
                recv_sem=sem_xr,
                device_id={"space": (y * NX + piece) * 2 + core},
                device_id_type=MESH,
            ).start()
        else:
            mine = both
    pltpu.make_async_copy(recv_x, recv_x, sem_xr).wait()
    for step in range(NX - 1):
        mine = mine + recv_x[step].astype(F32)

    send_z[...] = mine.astype(WIRE)
    n_zz = n_dp // 2
    holder = lax.rem(z, 2) == core

    def push_z(k, carry):
        slot = lax.rem(z // 2 + k, n_zz)

        @pl.when(2 * slot + core != z)
        def _():
            pltpu.make_async_remote_copy(
                src_ref=send_z.at[slot],
                dst_ref=recv_z.at[z],
                send_sem=sem_zs,
                recv_sem=sem_zr,
                device_id={"dp": 2 * slot + core},
                device_id_type=MESH,
            ).start()

        return carry

    lax.fori_loop(0, n_zz, push_z, 0)

    @pl.when(holder)
    def _():
        own = pltpu.make_async_copy(send_z.at[z // 2], recv_z.at[z], sem_own.at[2])
        own.start()
        own.wait()
        rest = recv_z.at[pl.ds(0, n_dp - 1)]
        pltpu.make_async_copy(rest, rest, sem_zr).wait()
        part_sum = recv_z[0].astype(F32)
        for step in range(1, n_dp):
            part_sum = part_sum + recv_z[step].astype(F32)
        recv_y[y] = part_sum
        copies = []
        for step in range(1, n_y):
            copy = pltpu.make_async_remote_copy(
                src_ref=recv_y.at[y],
                dst_ref=recv_y.at[y],
                send_sem=sem_ys,
                recv_sem=sem_yr,
                device_id={"space": (lax.rem(y + step, n_y) * NX + x) * 2 + core},
                device_id_type=MESH,
            )
            copy.start()
        if n_y > 1:
            rest_y = recv_y.at[pl.ds(0, n_y - 1)]
            pltpu.make_async_copy(rest_y, rest_y, sem_yr).wait()
        final = recv_y[0]
        for step in range(1, n_y):
            final = final + recv_y[step]
        recv_g[x] = final * norm
        for step in range(1, 2 * NX):
            other = lax.rem(2 * x + core + step, 2 * NX)
            pltpu.make_async_remote_copy(
                src_ref=recv_g.at[x],
                dst_ref=recv_g.at[x],
                send_sem=sem_gs,
                recv_sem=sem_gr,
                device_id={"space": y * 2 * NX + other},
                device_id_type=MESH,
            ).start()

    own_b.wait()
    others_b = recv_b.at[pl.ds(0, n_space - 1)]
    pltpu.make_async_copy(others_b, others_b, sem_br).wait()
    lat_modes = recv_b[...].reshape(rows, HALF)
    for half in range(2):
        field = (dot(inv_v[half], lat_modes) * scale).astype(BF16)
        out_field[:, :, half * HALF : (half + 1) * HALF] = field.reshape(LON, 2, HALF)

    @pl.when(holder)
    def _():
        got = recv_g.at[pl.ds(0, NX - 1)]
        pltpu.make_async_copy(got, got, sem_gr).wait()

    @pl.when(jnp.logical_not(holder))
    def _():
        pltpu.make_async_copy(recv_g, recv_g, sem_gr).wait()

    for group in range(6):
        first, second, third = (
            recv_g[(group * 3 + which) // PIECE, (group * 3 + which) % PIECE]
            for which in range(3)
        )
        at = slice(group * 8, group * 8 + 8)
        out_w1[0, at, :] = first[:, 0:BS]
        out_w1[1, at, :] = pltpu.roll(jnp.where(lane8 >= 96, first, second), 32, 1)[:, 0:BS]
        out_w2[0, at, :] = pltpu.roll(jnp.where(lane8 >= 64, second, third), 64, 1)[:, 0:BS]
        out_w2[1, at, :] = pltpu.roll(third, 96, 1)[:, 0:BS]
    tile = recv_g[18 // PIECE, 18 % PIECE]
    first, second, third = (
        jnp.broadcast_to(tile[which : which + 1], (8, LANES)) for which in range(3)
    )
    lines = (
        first,
        pltpu.roll(jnp.where(lane8 >= 96, first, second), 32, 1),
        pltpu.roll(jnp.where(lane8 >= 64, second, third), 64, 1),
        pltpu.roll(third, 96, 1),
    )
    odd = lax.rem(z, 2) == 1
    for index, line in enumerate(lines):
        line = jnp.where(odd, pltpu.roll(line, 80, 1), line)[0:1, 0:48]
        target = out_b1 if index < 2 else out_b2
        target[index % 2 : index % 2 + 1, :] = line

    def drained(ref, count, sem):
        part = ref.at[pl.ds(0, count)]
        pltpu.make_async_copy(part, part, sem).wait()

    drained(send_f, n_space - 1, sem_fs)
    drained(send_b, n_space - 1, sem_bs)
    drained(send_x, NX - 1, sem_xs)

    @pl.when(holder)
    def _():
        drained(send_z, n_zz - 1, sem_zs)
        if n_y > 1:
            drained(recv_y, n_y - 1, sem_ys)
        for _ in range(2 * NX - 1):
            drained(recv_g, 1, sem_gs)

    @pl.when(jnp.logical_not(holder))
    def _():
        drained(send_z, n_zz, sem_zs)


def per_device(activations, cotangent, w_first, w_second, b_first, lon_keep, relu_mask, shrink_mask):
    n_dp, n_space = lax.axis_size("dp"), lax.axis_size("space")
    lat_len = 2 * n_space
    rows = 8 * n_space
    n_y = n_space // (2 * NX)
    latf, latb = lat_constant(lat_len)
    flat_mask = (lat_len * 12, LANES)
    args = (
        lon_keep,
        lon_keep.reshape(1, n_space),
        jnp.swapaxes(activations[0], 0, 1),
        jnp.swapaxes(cotangent[0], 0, 1),
        jnp.swapaxes(w_first, 1, 2),
        jnp.swapaxes(w_second, 1, 2),
        b_first,
        relu_mask.reshape(flat_mask),
        shrink_mask.reshape(flat_mask),
        jnp.asarray(lon_constant()),
        jnp.asarray(latf),
        jnp.asarray(latb),
        jnp.asarray(spread_constant()),
    )
    anywhere = pl.BlockSpec(memory_space=pl.ANY)
    vmem = pl.BlockSpec(memory_space=pltpu.VMEM)
    dma = pltpu.SemaphoreType.DMA
    field, w1, w2, b1, b2 = pl.pallas_call(
        functools.partial(kernel, n_dp, n_space),
        out_shape=(
            jax.ShapeDtypeStruct((LON, 2, C), BF16),
            jax.ShapeDtypeStruct((2, 48, BS), F32),
            jax.ShapeDtypeStruct((2, 48, BS), F32),
            jax.ShapeDtypeStruct((2, 48), F32),
            jax.ShapeDtypeStruct((2, 48), F32),
        ),
        in_specs=[pl.BlockSpec(memory_space=pltpu.SMEM), vmem] + [anywhere] * 11,
        out_specs=(vmem,) * 5,
        scratch_shapes=[
            pltpu.VMEM((2, LON, 2, C), BF16),
            pltpu.VMEM(flat_mask, jnp.int32),
            pltpu.VMEM(flat_mask, jnp.int32),
            pltpu.VMEM((2, 2, BS, C), BF16),
            pltpu.VMEM((2, C), F32),
            pltpu.VMEM((2 * LON, 4 * LANES), BF16),
            pltpu.VMEM(latf.shape, BF16),
            pltpu.VMEM(latb.shape, BF16),
            pltpu.VMEM((HALF, 4 * LANES), BF16),
            dma((11,)),
            pltpu.VMEM((2, 2 * LON, rows), BF16),
            pltpu.VMEM((lat_len, 2048), F32),
            pltpu.VMEM((lat_len, 2048), F32),
            pltpu.VMEM((2, BLOCKS, 256, 256), BF16),
            pltpu.VMEM((8, 2048), F32),
            pltpu.VMEM((n_space, 8, C), BF16),
            pltpu.VMEM((n_space, 8, C), BF16),
            pltpu.VMEM((2 * lat_len, 1024), BF16),
            pltpu.VMEM((n_space, 8, HALF), BF16),
            pltpu.VMEM((n_space, 8, HALF), BF16),
            pltpu.VMEM((2, NX, BLOCKS, PIECE, ROWS, LANES), F32),
            pltpu.VMEM((NX, BLOCKS, PIECE, ROWS, LANES), F32),
            pltpu.VMEM((NX - 1, BLOCKS, PIECE, ROWS, LANES), WIRE),
            pltpu.VMEM((NX - 1, BLOCKS, PIECE, ROWS, LANES), WIRE),
            pltpu.VMEM((BLOCKS, PIECE, ROWS, LANES), WIRE),
            pltpu.VMEM((n_dp, PIECE, ROWS, LANES), WIRE),
            pltpu.VMEM((n_y, PIECE, ROWS, LANES), F32),
            pltpu.VMEM((NX, PIECE, ROWS, LANES), F32),
            dma,
            dma,
            dma,
            dma,
            dma((NX,)),
            dma((NX,)),
            dma,
            dma,
            dma,
            dma,
            dma,
            dma,
            dma,
            dma,
            dma((3,)),
        ],
        compiler_params=pltpu.CompilerParams(
            collective_id=0, has_side_effects=True, vmem_limit_bytes=48 << 20
        ),
    )(*args)
    return jnp.swapaxes(field, 0, 1)[None], w1, w2, b1, b2


def solution(mesh):
    return jax.shard_map(
        per_device,
        mesh=mesh,
        in_specs=(
            P("dp", "space", None, None),
            P("dp", "space", None, None),
            P(),
            P(),
            P(),
            P(),
            P("dp", None, None, "space", None),
            P("dp", None, None, "space", None),
        ),
        out_specs=(
            P("dp", "space", None, None),
            P(None, "dp", None),
            P(None, "dp", None),
            P(None, "dp"),
            P(None, "dp"),
        ),
        check_vma=False,
    )
```

```python
import functools
import math

import jax
import jax.numpy as jnp
import ml_dtypes
import numpy as np
from jax import lax
from jax.experimental import pallas as pl
from jax.experimental.pallas import tpu as pltpu
from jax.sharding import PartitionSpec as P

C = 768
BLOCKS = 8
LON = 180
BS = 96
HALF = C // 2
LANES = 128
NX = 4
ROWS = 8
TILES = 20
PIECE = TILES // NX
MESH = pl.DeviceIdType.MESH
F32 = jnp.float32
BF16 = jnp.bfloat16
WIRE = BF16


def lat_constant(lat_len):
    index = np.arange(lat_len)
    angle = ((index[:, None] * index[None, :]) % lat_len) * (2.0 * math.pi / lat_len)
    cosine, sine = np.cos(angle), np.sin(angle)
    table = np.stack(
        [np.stack([cosine, sine], -1), np.stack([-sine, cosine], -1)], 1
    )
    table = table.transpose(1, 0, 2, 3).reshape(2 * lat_len, lat_len // 2, 4)
    wide = np.zeros((2, 2 * lat_len, lat_len // 2, 2, 4))
    for part in range(2):
        wide[part, :, :, part, :] = table
    wide = wide.reshape(2, 2 * lat_len, 4 * lat_len).astype(ml_dtypes.bfloat16)
    return wide, np.ascontiguousarray(wide.transpose(0, 2, 1))


def lon_constant():
    columns, freq = np.arange(LON), np.arange(LON // 2 + 1)
    phase = (columns[:, None] * freq[None, :]) % LON
    angle = phase.astype(np.float32) * np.float32(2.0 * math.pi / LON)
    table = np.zeros((LON, 2, 2, 2, LANES))
    for row in range(2):
        table[:, row, row, 0, : LON // 2 + 1] = np.cos(angle)
        table[:, row, row, 1, : LON // 2 + 1] = -np.sin(angle)
    return table.reshape(2 * LON, 4 * LANES).astype(ml_dtypes.bfloat16)


def spread_constant():
    spread = np.zeros((HALF, 4 * LANES))
    for block in range(4):
        for channel in range(BS):
            spread[block * BS + channel, block * LANES + channel] = 1.0
    return spread.astype(ml_dtypes.bfloat16)


def dot(lhs, rhs, lhs_dim=1, rhs_dim=0):
    return lax.dot_general(
        lhs, rhs, (((lhs_dim,), (rhs_dim,)), ((), ())), preferred_element_type=F32
    )


def kernel(
    n_dp,
    n_space,
    keep_h,
    keep_row_h,
    act_h,
    cot_h,
    w1_h,
    w2_h,
    bias_h,
    relu_h,
    shrink_h,
    lonc_h,
    latf_h,
    latb_h,
    spread_h,
    field_v,
    recv_g,
    keep_s,
    keep_v,
    x_v,
    relu_v,
    shrink_v,
    w_v,
    bias_v,
    lonc_v,
    latf_v,
    latb_v,
    spread_v,
    load_sem,
    inv_v,
    rmask,
    smask,
    wmat,
    bias_p,
    send_f,
    recv_f,
    gspec,
    send_b,
    recv_b,
    chunks,
    recv_c,
    kept,
    send_x,
    recv_x,
    send_z,
    recv_z,
    recv_y,
    sem_fs,
    sem_fr,
    sem_bs,
    sem_br,
    sem_cs,
    sem_cr,
    sem_xs,
    sem_xr,
    sem_zs,
    sem_zr,
    sem_ys,
    sem_yr,
    sem_gs,
    sem_gr,
    sem_own,
):
    lat_len = 2 * n_space
    n_y = n_space // (2 * NX)
    scale = 1.0 / math.sqrt(lat_len * LON)
    norm = 1.0 / math.sqrt(n_dp * lat_len * n_space)
    z = lax.axis_index("dp")
    me = lax.axis_index("space")
    core = lax.rem(me, 2)
    x = lax.rem(me // 2, NX)
    y = me // (2 * NX)
    barrier = pltpu.get_barrier_semaphore()

    def greet_space(k, carry):
        peer = lax.rem(me + k, n_space)
        pl.semaphore_signal(barrier, inc=1, device_id={"space": peer}, device_id_type=MESH)
        return carry

    def greet_dp(k, carry):
        peer = lax.rem(z + k, n_dp)
        pl.semaphore_signal(barrier, inc=1, device_id={"dp": peer}, device_id_type=MESH)
        return carry

    loads = [
        pltpu.make_async_copy(lonc_h, lonc_v, load_sem.at[0]),
        pltpu.make_async_copy(act_h, x_v.at[0], load_sem.at[1]),
        pltpu.make_async_copy(cot_h, x_v.at[1], load_sem.at[2]),
        pltpu.make_async_copy(spread_h, spread_v, load_sem.at[3]),
        pltpu.make_async_copy(relu_h, relu_v, load_sem.at[4]),
        pltpu.make_async_copy(shrink_h, shrink_v, load_sem.at[5]),
        pltpu.make_async_copy(w1_h, w_v.at[0], load_sem.at[6]),
        pltpu.make_async_copy(w2_h, w_v.at[1], load_sem.at[7]),
        pltpu.make_async_copy(bias_h, bias_v, load_sem.at[8]),
        pltpu.make_async_copy(latf_h, latf_v, load_sem.at[9]),
        pltpu.make_async_copy(latb_h, latb_v, load_sem.at[10]),
        pltpu.make_async_copy(keep_h, keep_s, load_sem.at[11]),
        pltpu.make_async_copy(keep_row_h, keep_v, load_sem.at[12]),
    ]
    for load in loads:
        load.start()
    lax.fori_loop(1, n_space, greet_space, 0)
    lax.fori_loop(1, n_dp, greet_dp, 0)

    loads[12].wait()
    rows = 8 * n_space
    freq = lax.broadcasted_iota(jnp.int32, (LANES, n_space), 0)
    picked = jnp.where(freq == keep_v[...], 1.0, 0.0).astype(BF16)
    row_mode = lax.broadcasted_iota(jnp.int32, (rows, n_space), 0) >> 3
    mode = lax.broadcasted_iota(jnp.int32, (rows, n_space), 1)
    repeat = jnp.where(row_mode == mode, 1.0, 0.0).astype(BF16)
    one_hot = dot(repeat, picked, 1, 1)
    row_kind = lax.broadcasted_iota(jnp.int32, (rows, LANES), 0) & 3
    one_hot = jnp.concatenate(
        [jnp.where(row_kind == kind, one_hot, 0.0) for kind in range(4)], axis=1
    ).astype(BF16)
    loads[0].wait()
    lon_fwd = dot(one_hot, lonc_v[...], 1, 1)
    row_group = (lax.broadcasted_iota(jnp.int32, (rows, 2 * LON), 0) >> 2) & 1
    tables = []
    for part in range(2):
        loads[1 + part].wait()
        tables.append(jnp.where(row_group == part, lon_fwd, 0.0).astype(BF16))

    own_f = []
    for half in range(2):
        cut = slice(half * HALF, (half + 1) * HALF)
        total = dot(tables[0], x_v[0, :, :, cut].reshape(2 * LON, HALF)) + dot(
            tables[1], x_v[1, :, :, cut].reshape(2 * LON, HALF)
        )
        send_f[half] = total.astype(BF16).reshape(n_space, 8, HALF)
        if half == 0:
            pl.semaphore_wait(barrier, n_space + n_dp - 2)

        def push_forward(k, carry, half=half):
            peer = lax.rem(me + k, n_space)
            pltpu.make_async_remote_copy(
                src_ref=send_f.at[half, peer],
                dst_ref=recv_f.at[half, me],
                send_sem=sem_fs.at[half],
                recv_sem=sem_fr.at[half],
                device_id={"space": peer},
                device_id_type=MESH,
            ).start()
            return carry

        lax.fori_loop(1, n_space, push_forward, 0)
        own = pltpu.make_async_copy(send_f.at[half, me], recv_f.at[half, me], sem_own.at[half])
        own.start()
        own_f.append(own)

    loads[3].wait()
    spread = spread_v[...]
    spread_wide = spread.astype(F32)
    for load in loads[4:9]:
        load.wait()

    def prepare(half):
        cut = slice(half * HALF, (half + 1) * HALF)
        for source, target in ((relu_v, rmask), (shrink_v, smask)):
            for part in range(2):
                tiles = [
                    source[pl.ds(part * 6 + half * 3 + tile, lat_len, stride=12), :]
                    for tile in range(3)
                ]
                bits = jnp.concatenate(tiles, axis=1)
                bits = jnp.where(bits > 0, 1.0, 0.0).astype(BF16)
                wide = dot(bits, spread)
                for block in range(4):
                    target[:, pl.ds((half * 4 + block) * 256 + part * LANES, LANES)] = wide[
                        :, block * LANES : (block + 1) * LANES
                    ]
        for which in range(2):
            for part in range(2):
                wide = dot(w_v[which, part, :, cut], spread)
                for block in range(4):
                    tile = wide[:, block * LANES : (block + 1) * LANES].astype(BF16)
                    at = half * 4 + block
                    if part == 0:
                        wmat[which, at] = jnp.zeros((256, 256), BF16)
                        wmat[which, at, 0:BS, 0:LANES] = tile
                        wmat[which, at, LANES : LANES + BS, LANES:] = tile
                    else:
                        wmat[which, at, LANES : LANES + BS, 0:LANES] = tile
                        wmat[which, at, 0:BS, LANES:] = -tile
        for part in range(2):
            row = jnp.broadcast_to(bias_v[part : part + 1, cut], (8, HALF))
            wide = lax.dot_general(
                row,
                spread_wide,
                (((1,), (0,)), ((), ())),
                precision=lax.Precision.HIGHEST,
                preferred_element_type=F32,
            )
            for block in range(4):
                bias_p[:, pl.ds((half * 4 + block) * 256 + part * LANES, LANES)] = wide[
                    :, block * LANES : (block + 1) * LANES
                ]

    prepare(0)
    loads[9].wait()
    loads[10].wait()
    loads[11].wait()
    own_keep = keep_s[me]
    weight = jnp.where((own_keep == 0) | (2 * own_keep == LON), 1.0, 2.0).astype(F32)

    lane = lax.broadcasted_iota(jnp.int32, (BS, LANES), 1)
    lane8 = lax.broadcasted_iota(jnp.int32, (8, LANES), 1)
    row8 = lax.broadcasted_iota(jnp.int32, (8, LANES), 0)
    def packed(values, lanes):
        first = pltpu.roll(values[1], 96, 1)
        second = pltpu.roll(values[2], 64, 1)
        third = pltpu.roll(values[3], 32, 1)
        return (
            jnp.where(lanes < 96, values[0], first),
            jnp.where(lanes < 64, first, second),
            jnp.where(lanes < 32, second, third),
        )

    def spectral(half):
        own_f[half].wait()
        others = recv_f.at[half, pl.ds(0, n_space - 1)]
        pltpu.make_async_copy(others, others, sem_fr.at[half]).wait()
        modes = recv_f[half].reshape(rows, HALF)
        spec = [(dot(latf_v[part], modes) * scale).astype(BF16) for part in range(2)]
        wide_act = dot(spec[0], spread).astype(BF16)
        wide_cot = dot(spec[1], spread)
        for block in range(4):
            at = half * 4 + block
            lanes = slice(block * LANES, (block + 1) * LANES)
            span = slice(at * 256, (at + 1) * 256)
            zed = jnp.concatenate(
                [wide_act[0:lat_len, lanes], wide_act[lat_len:, lanes]], axis=1
            )
            cot = jnp.concatenate(
                [wide_cot[0:lat_len, lanes], wide_cot[lat_len:, lanes]], axis=1
            )
            gate = rmask[:, span] > 0.5
            grad_out = jnp.where(smask[:, span] > 0.5, weight * cot, 0.0).astype(BF16)
            pre = dot(zed, wmat[0, at], 1, 1) + bias_p[0:1, span]
            hidden = jnp.where(gate, pre, 0.0).astype(BF16)
            grad_hidden = dot(grad_out, wmat[1, at])
            grad_pre = jnp.where(gate, grad_hidden, 0.0).astype(BF16)
            grad_spec = dot(grad_pre, wmat[0, at]).astype(BF16)
            gspec[0:lat_len, pl.ds(at * LANES, LANES)] = grad_spec[:, 0:LANES]
            gspec[lat_len:, pl.ds(at * LANES, LANES)] = grad_spec[:, LANES:]
            outer = []
            for left, right in ((zed, grad_pre), (hidden, grad_out)):
                full = dot(left, right, 0, 0)
                outer.append(full[0:BS, 0:LANES] + full[LANES : LANES + BS, LANES:])
                outer.append(full[0:BS, LANES:] - full[LANES : LANES + BS, 0:LANES])
            tiles = packed(outer, lane)
            for parity in range(2):
                for group in range(6):
                    for which in range(3):
                        tile = group * 3 + which
                        start = parity * 48 + group * 8
                        chunks[half, parity, tile // PIECE, block, tile % PIECE] = tiles[which][
                            start : start + 8
                        ]
            sums = []
            for value in (grad_pre, grad_out):
                line = jnp.sum(value.astype(F32), axis=0, keepdims=True)
                sums.append(jnp.broadcast_to(line[:, 0:LANES], (8, LANES)))
                sums.append(jnp.broadcast_to(line[:, LANES:], (8, LANES)))
            lines = packed(sums, lane8)
            tile = jnp.where(
                row8 == 0, lines[0], jnp.where(row8 == 1, lines[1], jnp.where(row8 == 2, lines[2], 0.0))
            )
            for parity in range(2):
                chunks[half, parity, 18 // PIECE, block, 18 % PIECE] = tile
                chunks[half, parity, 19 // PIECE, block, 19 % PIECE] = jnp.zeros((8, LANES), F32)

    sibling = me + 1 - 2 * core
    n_zz = n_dp // 2
    holder = lax.rem(z, 2) == core
    core_copies = [[], []]

    def core_send(half):
        for step in range(NX):
            piece = lax.rem(x + 1 + step, NX)
            copy = pltpu.make_async_remote_copy(
                src_ref=chunks.at[half, 1 - core, piece],
                dst_ref=recv_c.at[half, piece],
                send_sem=sem_cs.at[half, step],
                recv_sem=sem_cr.at[half, step],
                device_id={"space": sibling},
                device_id_type=MESH,
            )
            copy.start()
            core_copies[half].append(copy)

    def x_send(half):
        for step in range(NX):
            piece = lax.rem(x + 1 + step, NX)
            core_copies[half][step].wait()
            both = chunks[half, core, piece] + recv_c[half, piece]
            if step < NX - 1:
                send_x[half, step] = both.astype(WIRE)
                pltpu.make_async_remote_copy(
                    src_ref=send_x.at[half, step],
                    dst_ref=recv_x.at[half, NX - 2 - step],
                    send_sem=sem_xs.at[half],
                    recv_sem=sem_xr.at[half],
                    device_id={"space": (y * NX + piece) * 2 + core},
                    device_id_type=MESH,
                ).start()
            else:
                kept[half] = both

    def z_send(half):
        pltpu.make_async_copy(recv_x.at[half], recv_x.at[half], sem_xr.at[half]).wait()
        mine = kept[half]
        for step in range(NX - 1):
            mine = mine + recv_x[half, step].astype(F32)
        send_z[half] = mine.astype(WIRE)
        for step in range(n_zz // 2):
            slot = lax.rem(z // 2 + step, n_zz // 2)
            plane = n_dp // 2 * half + 2 * slot + core

            @pl.when(plane != z)
            def _():
                pltpu.make_async_remote_copy(
                    src_ref=send_z.at[half, slot],
                    dst_ref=recv_z.at[z],
                    send_sem=sem_zs,
                    recv_sem=sem_zr,
                    device_id={"dp": plane},
                    device_id_type=MESH,
                ).start()

    spectral(0)
    core_send(0)
    prepare(1)
    x_send(0)
    spectral(1)
    core_send(1)
    z_send(0)
    x_send(1)

    grad_lat = None
    for half in range(2):
        narrow = dot(gspec[:, half * 512 : (half + 1) * 512], spread, 1, 1).astype(BF16)
        term = dot(latb_v[half], narrow)
        grad_lat = term if grad_lat is None else grad_lat + term
    send_b[...] = grad_lat.astype(BF16).reshape(n_space, 8, HALF)

    def push_back(k, carry):
        peer = lax.rem(me + k, n_space)
        pltpu.make_async_remote_copy(
            src_ref=send_b.at[peer],
            dst_ref=recv_b.at[me],
            send_sem=sem_bs,
            recv_sem=sem_br,
            device_id={"space": peer},
            device_id_type=MESH,
        ).start()
        return carry

    lax.fori_loop(1, n_space, push_back, 0)
    own_b = pltpu.make_async_copy(send_b.at[me], recv_b.at[me], sem_own.at[2])
    own_b.start()
    z_send(1)

    lon_inv = dot(lonc_v[...], one_hot, 1, 1)
    col_group = (lax.broadcasted_iota(jnp.int32, (2 * LON, rows), 1) >> 2) & 1
    for half in range(2):
        inv_v[half] = jnp.where(col_group == half, lon_inv, 0.0).astype(BF16)

    @pl.when(holder)
    def _():
        own = pltpu.make_async_copy(
            send_z.at[z // n_zz, lax.rem(z, n_zz) // 2], recv_z.at[z], sem_own.at[3]
        )
        own.start()
        own.wait()
        rest = recv_z.at[pl.ds(0, n_dp - 1)]
        pltpu.make_async_copy(rest, rest, sem_zr).wait()
        part_sum = recv_z[0].astype(F32)
        for step in range(1, n_dp):
            part_sum = part_sum + recv_z[step].astype(F32)
        recv_y[y] = part_sum.astype(WIRE)
        for step in range(1, n_y):
            pltpu.make_async_remote_copy(
                src_ref=recv_y.at[y],
                dst_ref=recv_y.at[y],
                send_sem=sem_ys,
                recv_sem=sem_yr,
                device_id={"space": (lax.rem(y + step, n_y) * NX + x) * 2 + core},
                device_id_type=MESH,
            ).start()
        rest_y = recv_y.at[pl.ds(0, n_y - 1)]
        pltpu.make_async_copy(rest_y, rest_y, sem_yr).wait()
        final = recv_y[0].astype(F32)
        for step in range(1, n_y):
            final = final + recv_y[step].astype(F32)
        recv_g[x] = final * norm
        for step in range(1, 2 * NX):
            other = lax.rem(2 * x + core + step, 2 * NX)
            pltpu.make_async_remote_copy(
                src_ref=recv_g.at[x],
                dst_ref=recv_g.at[x],
                send_sem=sem_gs,
                recv_sem=sem_gr,
                device_id={"space": y * 2 * NX + other},
                device_id_type=MESH,
            ).start()

    own_b.wait()
    others_b = recv_b.at[pl.ds(0, n_space - 1)]
    pltpu.make_async_copy(others_b, others_b, sem_br).wait()
    lat_modes = recv_b[...].reshape(rows, HALF)
    for half in range(2):
        field = (dot(inv_v[half], lat_modes) * scale).astype(BF16)
        field_v[:, :, half * HALF : (half + 1) * HALF] = field.reshape(LON, 2, HALF)

    @pl.when(holder)
    def _():
        got = recv_g.at[pl.ds(0, NX - 1)]
        pltpu.make_async_copy(got, got, sem_gr).wait()

    @pl.when(jnp.logical_not(holder))
    def _():
        pltpu.make_async_copy(recv_g, recv_g, sem_gr).wait()

    def drained(ref, count, sem):
        part = ref.at[pl.ds(0, count)]
        pltpu.make_async_copy(part, part, sem).wait()

    for half in range(2):
        drained(send_f.at[half], n_space - 1, sem_fs.at[half])
        drained(send_x.at[half], NX - 1, sem_xs.at[half])
    drained(send_b, n_space - 1, sem_bs)

    @pl.when(holder)
    def _():
        drained(recv_z, n_zz - 1, sem_zs)
        drained(recv_y, n_y - 1, sem_ys)
        for _ in range(2 * NX - 1):
            drained(recv_g, 1, sem_gs)

    @pl.when(jnp.logical_not(holder))
    def _():
        drained(recv_z, n_zz, sem_zs)


def finish(
    field_v,
    recv_g,
    field_h,
    w1_h,
    w2_h,
    b1_h,
    b2_h,
    out_w1,
    out_w2,
    out_b1,
    out_b2,
    sems,
):
    whole = pltpu.make_async_copy(field_v, field_h, sems.at[4])
    whole.start()
    z = lax.axis_index("dp")
    lane8 = lax.broadcasted_iota(jnp.int32, (8, LANES), 1)
    for group in range(6):
        first, second, third = (
            recv_g[(group * 3 + which) // PIECE, (group * 3 + which) % PIECE]
            for which in range(3)
        )
        at = slice(group * 8, group * 8 + 8)
        out_w1[0, at, :] = first[:, 0:BS]
        out_w1[1, at, :] = pltpu.roll(jnp.where(lane8 >= 96, first, second), 32, 1)[:, 0:BS]
        out_w2[0, at, :] = pltpu.roll(jnp.where(lane8 >= 64, second, third), 64, 1)[:, 0:BS]
        out_w2[1, at, :] = pltpu.roll(third, 96, 1)[:, 0:BS]
    tile = recv_g[18 // PIECE, 18 % PIECE]
    first, second, third = (
        jnp.broadcast_to(tile[which : which + 1], (8, LANES)) for which in range(3)
    )
    lines = (
        first,
        pltpu.roll(jnp.where(lane8 >= 96, first, second), 32, 1),
        pltpu.roll(jnp.where(lane8 >= 64, second, third), 64, 1),
        pltpu.roll(third, 96, 1),
    )
    odd = lax.rem(z, 2) == 1
    for index, line in enumerate(lines):
        line = jnp.where(odd, pltpu.roll(line, 80, 1), line)[0:1, 0:48]
        target = out_b1 if index < 2 else out_b2
        target[index % 2 : index % 2 + 1, :] = line
    small = [
        pltpu.make_async_copy(source, target, sems.at[index])
        for index, (source, target) in enumerate(
            ((out_w1, w1_h), (out_w2, w2_h), (out_b1, b1_h), (out_b2, b2_h))
        )
    ]
    for copy in small:
        copy.start()
    whole.wait()
    for copy in small:
        copy.wait()


def per_device(activations, cotangent, w_first, w_second, b_first, lon_keep, relu_mask, shrink_mask):
    n_dp, n_space = lax.axis_size("dp"), lax.axis_size("space")
    lat_len = 2 * n_space
    rows = 8 * n_space
    n_y = n_space // (2 * NX)
    latf, latb = lat_constant(lat_len)
    flat_mask = (lat_len * 12, LANES)
    args = (
        lon_keep,
        lon_keep.reshape(1, n_space),
        jnp.swapaxes(activations[0], 0, 1),
        jnp.swapaxes(cotangent[0], 0, 1),
        jnp.swapaxes(w_first, 1, 2),
        jnp.swapaxes(w_second, 1, 2),
        b_first,
        relu_mask.reshape(flat_mask),
        shrink_mask.reshape(flat_mask),
        jnp.asarray(lon_constant()),
        jnp.asarray(latf),
        jnp.asarray(latb),
        jnp.asarray(spread_constant()),
    )
    anywhere = pl.BlockSpec(memory_space=pltpu.HBM)
    vmem = pl.BlockSpec(memory_space=pltpu.VMEM)
    dma = pltpu.SemaphoreType.DMA
    got = pl.pallas_call(
        functools.partial(kernel, n_dp, n_space),
        out_shape=(
            jax.ShapeDtypeStruct((LON, 2, C), BF16),
            jax.ShapeDtypeStruct((NX, PIECE, ROWS, LANES), F32),
        ),
        in_specs=[anywhere] * 13,
        out_specs=(vmem,) * 2,
        scratch_shapes=[
            pltpu.SMEM((n_space,), jnp.int32),
            pltpu.VMEM((1, n_space), jnp.int32),
            pltpu.VMEM((2, LON, 2, C), BF16),
            pltpu.VMEM(flat_mask, jnp.int32),
            pltpu.VMEM(flat_mask, jnp.int32),
            pltpu.VMEM((2, 2, BS, C), BF16),
            pltpu.VMEM((2, C), F32),
            pltpu.VMEM((2 * LON, 4 * LANES), BF16),
            pltpu.VMEM(latf.shape, BF16),
            pltpu.VMEM(latb.shape, BF16),
            pltpu.VMEM((HALF, 4 * LANES), BF16),
            dma((13,)),
            pltpu.VMEM((2, 2 * LON, rows), BF16),
            pltpu.VMEM((lat_len, 2048), F32),
            pltpu.VMEM((lat_len, 2048), F32),
            pltpu.VMEM((2, BLOCKS, 256, 256), BF16),
            pltpu.VMEM((8, 2048), F32),
            pltpu.VMEM((2, n_space, 8, HALF), BF16),
            pltpu.VMEM((2, n_space, 8, HALF), BF16),
            pltpu.VMEM((2 * lat_len, 1024), BF16),
            pltpu.VMEM((n_space, 8, HALF), BF16),
            pltpu.VMEM((n_space, 8, HALF), BF16),
            pltpu.VMEM((2, 2, NX, 4, PIECE, ROWS, LANES), F32),
            pltpu.VMEM((2, NX, 4, PIECE, ROWS, LANES), F32),
            pltpu.VMEM((2, 4, PIECE, ROWS, LANES), F32),
            pltpu.VMEM((2, NX - 1, 4, PIECE, ROWS, LANES), WIRE),
            pltpu.VMEM((2, NX - 1, 4, PIECE, ROWS, LANES), WIRE),
            pltpu.VMEM((2, 4, PIECE, ROWS, LANES), WIRE),
            pltpu.VMEM((n_dp, PIECE, ROWS, LANES), WIRE),
            pltpu.VMEM((n_y, PIECE, ROWS, LANES), WIRE),
            dma((2,)),
            dma((2,)),
            dma,
            dma,
            dma((2, NX)),
            dma((2, NX)),
            dma((2,)),
            dma((2,)),
            dma,
            dma,
            dma,
            dma,
            dma,
            dma,
            dma((4,)),
        ],
        compiler_params=pltpu.CompilerParams(
            collective_id=0, has_side_effects=True, vmem_limit_bytes=48 << 20
        ),
    )(*(pltpu.with_memory_space_constraint(arg, pltpu.HBM) for arg in args))
    shapes = (
        jax.ShapeDtypeStruct((LON, 2, C), BF16),
        jax.ShapeDtypeStruct((2, 48, BS), F32),
        jax.ShapeDtypeStruct((2, 48, BS), F32),
        jax.ShapeDtypeStruct((2, 48), F32),
        jax.ShapeDtypeStruct((2, 48), F32),
    )
    field, w1, w2, b1, b2 = pl.pallas_call(
        finish,
        out_shape=shapes,
        in_specs=[vmem] * 2,
        out_specs=(anywhere,) * 5,
        scratch_shapes=[pltpu.VMEM(shape.shape, shape.dtype) for shape in shapes[1:]]
        + [dma((5,))],
        compiler_params=pltpu.CompilerParams(vmem_limit_bytes=16 << 20),
    )(*got)
    return jnp.swapaxes(field, 0, 1)[None], w1, w2, b1, b2


def solution(mesh):
    return jax.shard_map(
        per_device,
        mesh=mesh,
        in_specs=(
            P("dp", "space", None, None),
            P("dp", "space", None, None),
            P(),
            P(),
            P(),
            P(),
            P("dp", None, None, "space", None),
            P("dp", None, None, "space", None),
        ),
        out_specs=(
            P("dp", "space", None, None),
            P(None, "dp", None),
            P(None, "dp", None),
            P(None, "dp"),
            P(None, "dp"),
        ),
        check_vma=False,
    )
```

```python
import functools
import math

import jax
import jax.numpy as jnp
import ml_dtypes
import numpy as np
from jax import lax
from jax.experimental import pallas as pl
from jax.experimental.pallas import tpu as pltpu
from jax.sharding import PartitionSpec as P

C = 768
BLOCKS = 8
LON = 180
BS = 96
HALF = C // 2
LANES = 128
NX = 4
ROWS = 8
TILES = 20
PIECE = TILES // NX
MESH = pl.DeviceIdType.MESH
F32 = jnp.float32
BF16 = jnp.bfloat16
WIRE = BF16


def lat_constant(lat_len):
    index = np.arange(lat_len)
    angle = ((index[:, None] * index[None, :]) % lat_len) * (2.0 * math.pi / lat_len)
    cosine, sine = np.cos(angle), np.sin(angle)
    table = np.stack(
        [np.stack([cosine, sine], -1), np.stack([-sine, cosine], -1)], 1
    )
    table = table.transpose(1, 0, 2, 3).reshape(2 * lat_len, lat_len // 2, 4)
    wide = np.zeros((2, 2 * lat_len, lat_len // 2, 2, 4))
    for part in range(2):
        wide[part, :, :, part, :] = table
    wide = wide.reshape(2, 2 * lat_len, 4 * lat_len).astype(ml_dtypes.bfloat16)
    return wide, np.ascontiguousarray(wide.transpose(0, 2, 1))


def lon_constant():
    columns, freq = np.arange(LON), np.arange(LON // 2 + 1)
    phase = (columns[:, None] * freq[None, :]) % LON
    angle = phase.astype(np.float32) * np.float32(2.0 * math.pi / LON)
    table = np.zeros((LON, 2, 2, 2, LANES))
    for row in range(2):
        table[:, row, row, 0, : LON // 2 + 1] = np.cos(angle)
        table[:, row, row, 1, : LON // 2 + 1] = -np.sin(angle)
    return table.reshape(2 * LON, 4 * LANES).astype(ml_dtypes.bfloat16)


def spread_constant():
    spread = np.zeros((HALF, 4 * LANES))
    for block in range(4):
        for channel in range(BS):
            spread[block * BS + channel, block * LANES + channel] = 1.0
    return spread.astype(ml_dtypes.bfloat16)


def dot(lhs, rhs, lhs_dim=1, rhs_dim=0):
    return lax.dot_general(
        lhs, rhs, (((lhs_dim,), (rhs_dim,)), ((), ())), preferred_element_type=F32
    )


def kernel(
    n_dp,
    n_space,
    keep_h,
    keep_row_h,
    act_h,
    cot_h,
    w1_h,
    w2_h,
    bias_h,
    relu_h,
    shrink_h,
    lonc_h,
    latf_h,
    latb_h,
    spread_h,
    field_v,
    recv_g,
    keep_s,
    keep_v,
    x_v,
    relu_v,
    shrink_v,
    w_v,
    bias_v,
    lonc_v,
    latf_v,
    latb_v,
    spread_v,
    load_sem,
    inv_v,
    rmask,
    smask,
    wmat,
    bias_p,
    send_f,
    recv_f,
    gspec,
    send_b,
    recv_b,
    chunks,
    recv_c,
    kept,
    send_x,
    recv_x,
    send_z,
    recv_z,
    recv_y,
    sem_fs,
    sem_fr,
    sem_bs,
    sem_br,
    sem_cs,
    sem_cr,
    sem_xs,
    sem_xr,
    sem_zs,
    sem_zr,
    sem_ys,
    sem_yr,
    sem_gs,
    sem_gr,
    sem_own,
):
    lat_len = 2 * n_space
    n_y = n_space // (2 * NX)
    scale = 1.0 / math.sqrt(lat_len * LON)
    z = lax.axis_index("dp")
    me = lax.axis_index("space")
    core = lax.rem(me, 2)
    x = lax.rem(me // 2, NX)
    y = me // (2 * NX)
    barrier = pltpu.get_barrier_semaphore()

    def greet_space(k, carry):
        peer = lax.rem(me + k, n_space)
        pl.semaphore_signal(barrier, inc=1, device_id={"space": peer}, device_id_type=MESH)
        return carry

    def greet_dp(k, carry):
        peer = lax.rem(z + k, n_dp)
        pl.semaphore_signal(barrier, inc=1, device_id={"dp": peer}, device_id_type=MESH)
        return carry

    loads = [
        pltpu.make_async_copy(lonc_h, lonc_v, load_sem.at[0]),
        pltpu.make_async_copy(act_h, x_v.at[0], load_sem.at[1]),
        pltpu.make_async_copy(cot_h, x_v.at[1], load_sem.at[2]),
        pltpu.make_async_copy(spread_h, spread_v, load_sem.at[3]),
        pltpu.make_async_copy(relu_h, relu_v, load_sem.at[4]),
        pltpu.make_async_copy(shrink_h, shrink_v, load_sem.at[5]),
        pltpu.make_async_copy(w1_h, w_v.at[0], load_sem.at[6]),
        pltpu.make_async_copy(w2_h, w_v.at[1], load_sem.at[7]),
        pltpu.make_async_copy(bias_h, bias_v, load_sem.at[8]),
        pltpu.make_async_copy(latf_h, latf_v, load_sem.at[9]),
        pltpu.make_async_copy(latb_h, latb_v, load_sem.at[10]),
        pltpu.make_async_copy(keep_h, keep_s, load_sem.at[11]),
        pltpu.make_async_copy(keep_row_h, keep_v, load_sem.at[12]),
    ]
    urgent = (12, 0, 1, 2)
    for index in urgent:
        loads[index].start()
    lax.fori_loop(1, n_space, greet_space, 0, unroll=True)
    lax.fori_loop(1, n_dp, greet_dp, 0, unroll=True)
    for index, load in enumerate(loads):
        if index not in urgent:
            load.start()

    loads[12].wait()
    rows = 8 * n_space
    freq = lax.broadcasted_iota(jnp.int32, (LANES, n_space), 0)
    picked = jnp.where(freq == keep_v[...], 1.0, 0.0).astype(BF16)
    row_mode = lax.broadcasted_iota(jnp.int32, (rows, n_space), 0) >> 3
    mode = lax.broadcasted_iota(jnp.int32, (rows, n_space), 1)
    repeat = jnp.where(row_mode == mode, 1.0, 0.0).astype(BF16)
    one_hot = dot(repeat, picked, 1, 1)
    row_kind = lax.broadcasted_iota(jnp.int32, (rows, LANES), 0) & 3
    one_hot = jnp.concatenate(
        [jnp.where(row_kind == kind, one_hot, 0.0) for kind in range(4)], axis=1
    ).astype(BF16)
    loads[0].wait()
    lon_fwd = dot(one_hot, lonc_v[...], 1, 1)
    row_group = (lax.broadcasted_iota(jnp.int32, (rows, 2 * LON), 0) >> 2) & 1
    tables = []
    for part in range(2):
        loads[1 + part].wait()
        tables.append(jnp.where(row_group == part, lon_fwd, 0.0).astype(BF16))

    own_f = []
    for half in range(2):
        cut = slice(half * HALF, (half + 1) * HALF)
        total = dot(tables[0], x_v[0, :, :, cut].reshape(2 * LON, HALF)) + dot(
            tables[1], x_v[1, :, :, cut].reshape(2 * LON, HALF)
        )
        send_f[half] = total.astype(BF16).reshape(n_space, 8, HALF)
        if half == 0:
            pl.semaphore_wait(barrier, n_space + n_dp - 2)

        def push_forward(k, carry, half=half):
            peer = lax.rem(me + k, n_space)
            pltpu.make_async_remote_copy(
                src_ref=send_f.at[half, peer],
                dst_ref=recv_f.at[half, me],
                send_sem=sem_fs.at[half],
                recv_sem=sem_fr.at[half],
                device_id={"space": peer},
                device_id_type=MESH,
            ).start()
            return carry

        lax.fori_loop(1, n_space, push_forward, 0, unroll=7)
        own = pltpu.make_async_copy(send_f.at[half, me], recv_f.at[half, me], sem_own.at[half])
        own.start()
        own_f.append(own)

    loads[3].wait()
    spread = spread_v[...]
    spread_wide = spread.astype(F32)
    for load in loads[4:9]:
        load.wait()

    def prepare(half):
        cut = slice(half * HALF, (half + 1) * HALF)
        for source, target in ((relu_v, rmask), (shrink_v, smask)):
            for part in range(2):
                tiles = [
                    source[pl.ds(part * 6 + half * 3 + tile, lat_len, stride=12), :]
                    for tile in range(3)
                ]
                bits = jnp.concatenate(tiles, axis=1)
                bits = jnp.where(bits > 0, 1.0, 0.0).astype(BF16)
                wide = dot(bits, spread)
                for block in range(4):
                    target[:, pl.ds((half * 4 + block) * 256 + part * LANES, LANES)] = wide[
                        :, block * LANES : (block + 1) * LANES
                    ]
        for which in range(2):
            for part in range(2):
                wide = dot(w_v[which, part, :, cut], spread)
                for block in range(4):
                    tile = wide[:, block * LANES : (block + 1) * LANES].astype(BF16)
                    at = half * 4 + block
                    if part == 0:
                        wmat[which, at] = jnp.zeros((256, 256), BF16)
                        wmat[which, at, 0:BS, 0:LANES] = tile
                        wmat[which, at, LANES : LANES + BS, LANES:] = tile
                    else:
                        wmat[which, at, LANES : LANES + BS, 0:LANES] = tile
                        wmat[which, at, 0:BS, LANES:] = -tile
        for part in range(2):
            row = jnp.broadcast_to(bias_v[part : part + 1, cut], (8, HALF))
            wide = lax.dot_general(
                row,
                spread_wide,
                (((1,), (0,)), ((), ())),
                precision=lax.Precision.HIGHEST,
                preferred_element_type=F32,
            )
            for block in range(4):
                bias_p[:, pl.ds((half * 4 + block) * 256 + part * LANES, LANES)] = wide[
                    :, block * LANES : (block + 1) * LANES
                ]

    prepare(0)
    loads[9].wait()
    loads[10].wait()
    loads[11].wait()
    own_keep = keep_s[me]
    weight = jnp.where((own_keep == 0) | (2 * own_keep == LON), 1.0, 2.0).astype(F32)

    lane = lax.broadcasted_iota(jnp.int32, (BS, LANES), 1)
    lane8 = lax.broadcasted_iota(jnp.int32, (8, LANES), 1)
    row8 = lax.broadcasted_iota(jnp.int32, (8, LANES), 0)
    def packed(values, lanes):
        first = pltpu.roll(values[1], 96, 1)
        second = pltpu.roll(values[2], 64, 1)
        third = pltpu.roll(values[3], 32, 1)
        return (
            jnp.where(lanes < 96, values[0], first),
            jnp.where(lanes < 64, first, second),
            jnp.where(lanes < 32, second, third),
        )

    def spectral(half):
        own_f[half].wait()
        others = recv_f.at[half, pl.ds(0, n_space - 1)]
        pltpu.make_async_copy(others, others, sem_fr.at[half]).wait()
        modes = recv_f[half].reshape(rows, HALF)
        spec = [(dot(latf_v[part], modes) * scale).astype(BF16) for part in range(2)]
        wide_act = dot(spec[0], spread).astype(BF16)
        wide_cot = dot(spec[1], spread)
        for block in range(4):
            at = half * 4 + block
            lanes = slice(block * LANES, (block + 1) * LANES)
            span = slice(at * 256, (at + 1) * 256)
            zed = jnp.concatenate(
                [wide_act[0:lat_len, lanes], wide_act[lat_len:, lanes]], axis=1
            )
            cot = jnp.concatenate(
                [wide_cot[0:lat_len, lanes], wide_cot[lat_len:, lanes]], axis=1
            )
            gate = rmask[:, span] > 0.5
            grad_out = jnp.where(smask[:, span] > 0.5, weight * cot, 0.0).astype(BF16)
            pre = dot(zed, wmat[0, at], 1, 1) + bias_p[0:1, span]
            hidden = jnp.where(gate, pre, 0.0).astype(BF16)
            grad_hidden = dot(grad_out, wmat[1, at])
            grad_pre = jnp.where(gate, grad_hidden, 0.0).astype(BF16)
            grad_spec = dot(grad_pre, wmat[0, at]).astype(BF16)
            gspec[0:lat_len, pl.ds(at * LANES, LANES)] = grad_spec[:, 0:LANES]
            gspec[lat_len:, pl.ds(at * LANES, LANES)] = grad_spec[:, LANES:]
            outer = []
            for left, right in ((zed, grad_pre), (hidden, grad_out)):
                full = dot(left, right, 0, 0)
                outer.append(full[0:BS, 0:LANES] + full[LANES : LANES + BS, LANES:])
                outer.append(full[0:BS, LANES:] - full[LANES : LANES + BS, 0:LANES])
            tiles = packed(outer, lane)
            for parity in range(2):
                for group in range(6):
                    for which in range(3):
                        tile = group * 3 + which
                        start = parity * 48 + group * 8
                        chunks[half, parity, tile // PIECE, block, tile % PIECE] = tiles[which][
                            start : start + 8
                        ]
            sums = []
            for value in (grad_pre, grad_out):
                line = jnp.sum(value.astype(F32), axis=0, keepdims=True)
                sums.append(jnp.broadcast_to(line[:, 0:LANES], (8, LANES)))
                sums.append(jnp.broadcast_to(line[:, LANES:], (8, LANES)))
            lines = packed(sums, lane8)
            tile = jnp.where(
                row8 == 0, lines[0], jnp.where(row8 == 1, lines[1], jnp.where(row8 == 2, lines[2], 0.0))
            )
            for parity in range(2):
                chunks[half, parity, 18 // PIECE, block, 18 % PIECE] = tile
                chunks[half, parity, 19 // PIECE, block, 19 % PIECE] = jnp.zeros((8, LANES), F32)

    sibling = me + 1 - 2 * core
    n_zz = n_dp // 2
    holder = lax.rem(z, 2) == core
    core_copies = [[], []]

    def core_send(half):
        for step in range(NX):
            piece = lax.rem(x + 1 + step, NX)
            copy = pltpu.make_async_remote_copy(
                src_ref=chunks.at[half, 1 - core, piece],
                dst_ref=recv_c.at[half, piece],
                send_sem=sem_cs.at[half, step],
                recv_sem=sem_cr.at[half, step],
                device_id={"space": sibling},
                device_id_type=MESH,
            )
            copy.start()
            core_copies[half].append(copy)

    def x_send(half):
        for step in range(NX):
            piece = lax.rem(x + 1 + step, NX)
            core_copies[half][step].wait()
            both = chunks[half, core, piece] + recv_c[half, piece]
            if step < NX - 1:
                send_x[half, step] = both.astype(WIRE)
                pltpu.make_async_remote_copy(
                    src_ref=send_x.at[half, step],
                    dst_ref=recv_x.at[half, NX - 2 - step],
                    send_sem=sem_xs.at[half],
                    recv_sem=sem_xr.at[half],
                    device_id={"space": (y * NX + piece) * 2 + core},
                    device_id_type=MESH,
                ).start()
            else:
                kept[half] = both

    def z_send(half):
        pltpu.make_async_copy(recv_x.at[half], recv_x.at[half], sem_xr.at[half]).wait()
        mine = kept[half]
        for step in range(NX - 1):
            mine = mine + recv_x[half, step].astype(F32)
        send_z[half] = mine.astype(WIRE)
        for step in range(n_zz // 2):
            slot = lax.rem(z // 2 + step, n_zz // 2)
            plane = n_dp // 2 * half + 2 * slot + core

            @pl.when(plane != z)
            def _():
                pltpu.make_async_remote_copy(
                    src_ref=send_z.at[half, slot],
                    dst_ref=recv_z.at[z],
                    send_sem=sem_zs,
                    recv_sem=sem_zr,
                    device_id={"dp": plane},
                    device_id_type=MESH,
                ).start()

    spectral(0)
    core_send(0)
    prepare(1)
    x_send(0)
    lon_inv = dot(lonc_v[...], one_hot, 1, 1)
    col_group = (lax.broadcasted_iota(jnp.int32, (2 * LON, rows), 1) >> 2) & 1
    for half in range(2):
        inv_v[half] = jnp.where(col_group == half, lon_inv, 0.0).astype(BF16)
    spectral(1)
    core_send(1)
    z_send(0)
    x_send(1)

    grad_lat = None
    for half in range(2):
        narrow = dot(gspec[:, half * 512 : (half + 1) * 512], spread, 1, 1).astype(BF16)
        term = dot(latb_v[half], narrow)
        grad_lat = term if grad_lat is None else grad_lat + term
    send_b[...] = grad_lat.astype(BF16).reshape(n_space, 8, HALF)

    def push_back(k, carry):
        peer = lax.rem(me + k, n_space)
        pltpu.make_async_remote_copy(
            src_ref=send_b.at[peer],
            dst_ref=recv_b.at[me],
            send_sem=sem_bs,
            recv_sem=sem_br,
            device_id={"space": peer},
            device_id_type=MESH,
        ).start()
        return carry

    lax.fori_loop(1, n_space, push_back, 0, unroll=7)
    own_b = pltpu.make_async_copy(send_b.at[me], recv_b.at[me], sem_own.at[2])
    own_b.start()
    z_send(1)

    @pl.when(holder)
    def _():
        recv_z[z] = send_z[z // n_zz, lax.rem(z, n_zz) // 2]
        rest = recv_z.at[pl.ds(0, n_dp - 1)]
        pltpu.make_async_copy(rest, rest, sem_zr).wait()
        part_sum = recv_z[0].astype(F32)
        for step in range(1, n_dp):
            part_sum = part_sum + recv_z[step].astype(F32)
        recv_y[y] = part_sum.astype(WIRE)
        for step in range(1, n_y):
            pltpu.make_async_remote_copy(
                src_ref=recv_y.at[y],
                dst_ref=recv_y.at[y],
                send_sem=sem_ys,
                recv_sem=sem_yr,
                device_id={"space": (lax.rem(y + step, n_y) * NX + x) * 2 + core},
                device_id_type=MESH,
            ).start()
        rest_y = recv_y.at[pl.ds(0, n_y - 1)]
        pltpu.make_async_copy(rest_y, rest_y, sem_yr).wait()
        final = recv_y[0].astype(F32)
        for step in range(1, n_y):
            final = final + recv_y[step].astype(F32)
        recv_g[x] = final.astype(WIRE)
        for step in range(1, 2 * NX):
            other = lax.rem(2 * x + core + step, 2 * NX)
            pltpu.make_async_remote_copy(
                src_ref=recv_g.at[x],
                dst_ref=recv_g.at[x],
                send_sem=sem_gs,
                recv_sem=sem_gr,
                device_id={"space": y * 2 * NX + other},
                device_id_type=MESH,
            ).start()

    own_b.wait()
    others_b = recv_b.at[pl.ds(0, n_space - 1)]
    pltpu.make_async_copy(others_b, others_b, sem_br).wait()
    lat_modes = recv_b[...].reshape(rows, HALF)
    for half in range(2):
        field = (dot(inv_v[half], lat_modes) * scale).astype(BF16)
        field_v[:, :, half * HALF : (half + 1) * HALF] = field.reshape(LON, 2, HALF)

    @pl.when(holder)
    def _():
        got = recv_g.at[pl.ds(0, NX - 1)]
        pltpu.make_async_copy(got, got, sem_gr).wait()

    @pl.when(jnp.logical_not(holder))
    def _():
        pltpu.make_async_copy(recv_g, recv_g, sem_gr).wait()

    def drained(ref, count, sem):
        part = ref.at[pl.ds(0, count)]
        pltpu.make_async_copy(part, part, sem).wait()

    for half in range(2):
        drained(send_f.at[half], n_space - 1, sem_fs.at[half])
        drained(send_x.at[half], NX - 1, sem_xs.at[half])
    drained(send_b, n_space - 1, sem_bs)

    @pl.when(holder)
    def _():
        drained(recv_z, n_zz - 1, sem_zs)
        drained(recv_y, n_y - 1, sem_ys)
        for _ in range(2 * NX - 1):
            drained(recv_g, 1, sem_gs)

    @pl.when(jnp.logical_not(holder))
    def _():
        drained(recv_z, n_zz, sem_zs)


def finish(
    norm,
    field_v,
    recv_g,
    field_h,
    w1_h,
    w2_h,
    b1_h,
    b2_h,
    out_w1,
    out_w2,
    out_b1,
    out_b2,
    sems,
):
    whole = pltpu.make_async_copy(field_v, field_h, sems.at[4])
    whole.start()
    z = lax.axis_index("dp")
    lane8 = lax.broadcasted_iota(jnp.int32, (8, LANES), 1)
    for group in range(6):
        first, second, third = (
            recv_g[(group * 3 + which) // PIECE, (group * 3 + which) % PIECE].astype(F32) * norm
            for which in range(3)
        )
        at = slice(group * 8, group * 8 + 8)
        out_w1[0, at, :] = first[:, 0:BS]
        out_w1[1, at, :] = pltpu.roll(jnp.where(lane8 >= 96, first, second), 32, 1)[:, 0:BS]
        out_w2[0, at, :] = pltpu.roll(jnp.where(lane8 >= 64, second, third), 64, 1)[:, 0:BS]
        out_w2[1, at, :] = pltpu.roll(third, 96, 1)[:, 0:BS]
    tile = recv_g[18 // PIECE, 18 % PIECE].astype(F32) * norm
    first, second, third = (
        jnp.broadcast_to(tile[which : which + 1], (8, LANES)) for which in range(3)
    )
    lines = (
        first,
        pltpu.roll(jnp.where(lane8 >= 96, first, second), 32, 1),
        pltpu.roll(jnp.where(lane8 >= 64, second, third), 64, 1),
        pltpu.roll(third, 96, 1),
    )
    odd = lax.rem(z, 2) == 1
    for index, line in enumerate(lines):
        line = jnp.where(odd, pltpu.roll(line, 80, 1), line)[0:1, 0:48]
        target = out_b1 if index < 2 else out_b2
        target[index % 2 : index % 2 + 1, :] = line
    small = [
        pltpu.make_async_copy(source, target, sems.at[index])
        for index, (source, target) in enumerate(
            ((out_w1, w1_h), (out_w2, w2_h), (out_b1, b1_h), (out_b2, b2_h))
        )
    ]
    for copy in small:
        copy.start()
    whole.wait()
    for copy in small:
        copy.wait()


def per_device(activations, cotangent, w_first, w_second, b_first, lon_keep, relu_mask, shrink_mask):
    n_dp, n_space = lax.axis_size("dp"), lax.axis_size("space")
    lat_len = 2 * n_space
    rows = 8 * n_space
    n_y = n_space // (2 * NX)
    latf, latb = lat_constant(lat_len)
    flat_mask = (lat_len * 12, LANES)
    args = (
        lon_keep,
        lon_keep.reshape(1, n_space),
        jnp.swapaxes(activations[0], 0, 1),
        jnp.swapaxes(cotangent[0], 0, 1),
        jnp.swapaxes(w_first, 1, 2),
        jnp.swapaxes(w_second, 1, 2),
        b_first,
        relu_mask.reshape(flat_mask),
        shrink_mask.reshape(flat_mask),
        jnp.asarray(lon_constant()),
        jnp.asarray(latf),
        jnp.asarray(latb),
        jnp.asarray(spread_constant()),
    )
    anywhere = pl.BlockSpec(memory_space=pltpu.HBM)
    vmem = pl.BlockSpec(memory_space=pltpu.VMEM)
    dma = pltpu.SemaphoreType.DMA
    got = pl.pallas_call(
        functools.partial(kernel, n_dp, n_space),
        out_shape=(
            jax.ShapeDtypeStruct((LON, 2, C), BF16),
            jax.ShapeDtypeStruct((NX, PIECE, ROWS, LANES), WIRE),
        ),
        in_specs=[anywhere] * 13,
        out_specs=(vmem,) * 2,
        scratch_shapes=[
            pltpu.SMEM((n_space,), jnp.int32),
            pltpu.VMEM((1, n_space), jnp.int32),
            pltpu.VMEM((2, LON, 2, C), BF16),
            pltpu.VMEM(flat_mask, jnp.int32),
            pltpu.VMEM(flat_mask, jnp.int32),
            pltpu.VMEM((2, 2, BS, C), BF16),
            pltpu.VMEM((2, C), F32),
            pltpu.VMEM((2 * LON, 4 * LANES), BF16),
            pltpu.VMEM(latf.shape, BF16),
            pltpu.VMEM(latb.shape, BF16),
            pltpu.VMEM((HALF, 4 * LANES), BF16),
            dma((13,)),
            pltpu.VMEM((2, 2 * LON, rows), BF16),
            pltpu.VMEM((lat_len, 2048), F32),
            pltpu.VMEM((lat_len, 2048), F32),
            pltpu.VMEM((2, BLOCKS, 256, 256), BF16),
            pltpu.VMEM((8, 2048), F32),
            pltpu.VMEM((2, n_space, 8, HALF), BF16),
            pltpu.VMEM((2, n_space, 8, HALF), BF16),
            pltpu.VMEM((2 * lat_len, 1024), BF16),
            pltpu.VMEM((n_space, 8, HALF), BF16),
            pltpu.VMEM((n_space, 8, HALF), BF16),
            pltpu.VMEM((2, 2, NX, 4, PIECE, ROWS, LANES), F32),
            pltpu.VMEM((2, NX, 4, PIECE, ROWS, LANES), F32),
            pltpu.VMEM((2, 4, PIECE, ROWS, LANES), F32),
            pltpu.VMEM((2, NX - 1, 4, PIECE, ROWS, LANES), WIRE),
            pltpu.VMEM((2, NX - 1, 4, PIECE, ROWS, LANES), WIRE),
            pltpu.VMEM((2, 4, PIECE, ROWS, LANES), WIRE),
            pltpu.VMEM((n_dp, PIECE, ROWS, LANES), WIRE),
            pltpu.VMEM((n_y, PIECE, ROWS, LANES), WIRE),
            dma((2,)),
            dma((2,)),
            dma,
            dma,
            dma((2, NX)),
            dma((2, NX)),
            dma((2,)),
            dma((2,)),
            dma,
            dma,
            dma,
            dma,
            dma,
            dma,
            dma((3,)),
        ],
        compiler_params=pltpu.CompilerParams(
            collective_id=0, has_side_effects=True, vmem_limit_bytes=48 << 20
        ),
    )(*(pltpu.with_memory_space_constraint(arg, pltpu.HBM) for arg in args))
    shapes = (
        jax.ShapeDtypeStruct((LON, 2, C), BF16),
        jax.ShapeDtypeStruct((2, 48, BS), F32),
        jax.ShapeDtypeStruct((2, 48, BS), F32),
        jax.ShapeDtypeStruct((2, 48), F32),
        jax.ShapeDtypeStruct((2, 48), F32),
    )
    field, w1, w2, b1, b2 = pl.pallas_call(
        functools.partial(finish, 1.0 / math.sqrt(n_dp * lat_len * n_space)),
        out_shape=shapes,
        in_specs=[vmem] * 2,
        out_specs=(anywhere,) * 5,
        scratch_shapes=[pltpu.VMEM(shape.shape, shape.dtype) for shape in shapes[1:]]
        + [dma((5,))],
        compiler_params=pltpu.CompilerParams(vmem_limit_bytes=16 << 20),
    )(*got)
    return jnp.swapaxes(field, 0, 1)[None], w1, w2, b1, b2


def solution(mesh):
    return jax.shard_map(
        per_device,
        mesh=mesh,
        in_specs=(
            P("dp", "space", None, None),
            P("dp", "space", None, None),
            P(),
            P(),
            P(),
            P(),
            P("dp", None, None, "space", None),
            P("dp", None, None, "space", None),
        ),
        out_specs=(
            P("dp", "space", None, None),
            P(None, "dp", None),
            P(None, "dp", None),
            P(None, "dp"),
            P(None, "dp"),
        ),
        check_vma=False,
    )
```
